128 devices in a mesh: box: 4 (over z_hi, core), dir: 32 (over x, z_lo, y).
Axes of the slice: x: 4, y: 4, z: 4 (z_hi: 2, z_lo: 2; z = z_hi * 2 + z_lo), core: 2. Of those that a mesh axis runs over, the one named last changes fastest.
Arguments:
- fine_pattern: bfloat16 [512, 2, 16, 8192], P(('box', 'dir')), may hold values from -6 to 6
- fine_interp: bfloat16 [32, 384, 896], P('dir'), may hold values from -0.3125 to 0.3125
- mid_interp: bfloat16 [32, 1024, 3328], P('dir'), may hold values from -0.1875 to 0.1875
- fine_angle: float32 [8, 28672], P(None, 'dir'), may hold values from -3.140625 to 3.140625
- top_angle: float32 [8, 106496], P(None, 'dir'), may hold values from -3.140625 to 3.140625
- translator: bfloat16 [64, 2, 106496], P(None, None, 'dir'), may hold values from -1 to 1
- fine_position: int32 [512], replicated, may hold values from 0 to 7
- mid_position: int32 [128], replicated, may hold values from 0 to 7
- fine_parent: int32 [512], replicated, may hold values from 0 to 127, as said below
- mid_parent: int32 [128], replicated, may hold values from 0 to 31, as said below
- pair_target: int32 [256], replicated, may hold values from 0 to 31
- pair_source: int32 [256], replicated, may hold values from 0 to 31
- pair_kind: int32 [256], replicated, may hold values from 0 to 63
Outputs:
- top_incoming: float32 [32, 2, 16, 106496], P('box', None, None, 'dir')
- mid_incoming: float32 [128, 2, 16, 28672], P('box', None, None, 'dir')
The draws below stay inside these ranges and needn't reach their ends.
Inputs may be any that keep to these rules, and one draw needn't show every extreme that they name: `fine_parent`: for every k, the fine boxes k * 128 to (k + 1) * 128 - 1 have their parents among the middle boxes k * 32 to (k + 1) * 32 - 1, and every middle box has exactly 4 children. `mid_parent`: for every k, the middle boxes k * 32 to (k + 1) * 32 - 1 have their parents among the top boxes k * 8 to (k + 1) * 8 - 1, and every top box has exactly 4 children.
All inputs are finite; a program needn't handle non-finite values.
Results may differ from the reference program's by a relative error of at most 0.0072.
Values may be sent and summed in bfloat16 or wider, within the bound.
No kernel may reach another device: no remote copies, remote signals or barrier semaphores. Data moves between devices by JAX's collectives and lax.ppermute only.
A program may use at most 128 MiB of HBM per device.

```python
import jax
import jax.numpy as jnp
from jax import lax

RHS = 16
SECT = 32
FS = 256
MS = 896
TS = 3328
HALO = 64
POS = 8
KINDS = 64
FGROUP = 128
MGROUP = 32
FBOX = 512
MBOX = 128
TBOX = 32
FDIR = 8192
MDIR = 28672
TDIR = 106496
PAIRS = 256


def grouped_parents(key, count_all, per_group):
    groups = count_all // per_group
    group_keys = jax.random.split(key, groups)
    shuffled = jax.vmap(lambda single: jax.random.permutation(single, per_group))(group_keys)
    offsets = jnp.arange(groups, dtype=jnp.int32)[:, None] * (per_group // 4)
    return (offsets + shuffled.astype(jnp.int32) // 4).reshape(count_all).astype(jnp.int32)


def draw_fine_parent(key, part):
    return grouped_parents(jax.random.fold_in(key, 17), FBOX, FGROUP)


def draw_mid_parent(key, part):
    return grouped_parents(jax.random.fold_in(key, 29), MBOX, MGROUP)


def with_ends(values, key, low, largest):
    dims = values.shape
    index_at = [jax.random.randint(jax.random.fold_in(key, axis), (), 0, dims[axis]) for axis in range(len(dims))]
    values = values.at[tuple(index_at)].set(low)
    longest = dims.index(max(dims))
    index_at[longest] = (index_at[longest] + 1) % dims[longest]
    return values.at[tuple(index_at)].set(largest)


def level_of(key, shape, cuts, smallest, high):
    loudness, own = 1.0, jax.random.fold_in(key, 6)
    for position, blocks in cuts:
        steps = jnp.exp(jax.random.uniform(jax.random.fold_in(own, position), (blocks,), jnp.float32, smallest / len(cuts), high / len(cuts)))
        loudness = loudness * jnp.repeat(steps, shape[position] // blocks).reshape([-1 if axis == position else 1 for axis in range(len(shape))])
    return loudness


def normal_values(rng, shape, scale, bound, cuts=(), kind=jnp.bfloat16):
    drawn = jax.random.normal(rng, shape, jnp.float32) * scale
    if len(cuts) > 0:
        drawn = level_of(rng, shape, cuts, -0.22, 0.18) * drawn
    return jnp.clip(drawn, min=-bound, max=bound).astype(kind)


def setup_inputs(seed: int = 0) -> dict:
    key_of = jax.random.split(jax.random.key(seed), 14)
    fine_pattern = normal_values(key_of[0], (FBOX, 2, RHS, FDIR), 1.0, 6.0, ((0, 128),))
    fine_interp = normal_values(key_of[1], (SECT, FS + 2 * HALO, MS), (FS + 2 * HALO) ** -0.5, 0.3125, ((0, 32),))
    mid_interp = normal_values(key_of[2], (SECT, MS + 2 * HALO, TS), (MS + 2 * HALO) ** -0.5, 0.1875, ((0, 32),))
    fine_angle = jnp.clip(jax.random.uniform(key_of[3], (POS, MDIR), jnp.float32, -3.140625, 3.140625), -3.140625, 3.140625)
    top_angle = jnp.clip(jax.random.uniform(key_of[4], (POS, TDIR), jnp.float32, -3.140625, 3.140625), -3.140625, 3.140625)
    translator = normal_values(key_of[5], (KINDS, 2, TDIR), 0.15, 1.0, ((2, 32),))
    fine_position = with_ends(jax.random.randint(key_of[6], (FBOX,), 0, POS), jax.random.fold_in(key_of[6], 1), 0, POS - 1).astype(jnp.int32)
    mid_position = with_ends(jax.random.randint(key_of[7], (MBOX,), 0, POS), jax.random.fold_in(key_of[7], 1), 0, POS - 1).astype(jnp.int32)
    fine_parent = draw_fine_parent(jax.random.fold_in(key_of[13], 71), 0)
    mid_parent = draw_mid_parent(jax.random.fold_in(key_of[13], 71), 0)
    pair_target = with_ends(jax.random.randint(key_of[10], (PAIRS,), 0, TBOX), jax.random.fold_in(key_of[10], 1), 0, TBOX - 1).astype(jnp.int32)
    pair_source = with_ends(jax.random.randint(key_of[11], (PAIRS,), 0, TBOX), jax.random.fold_in(key_of[11], 1), 0, TBOX - 1).astype(jnp.int32)
    pair_kind = with_ends(jax.random.randint(key_of[12], (PAIRS,), 0, KINDS), jax.random.fold_in(key_of[12], 1), 0, KINDS - 1).astype(jnp.int32)
    return dict(fine_pattern=fine_pattern, fine_interp=fine_interp, mid_interp=mid_interp, fine_angle=fine_angle, top_angle=top_angle, translator=translator, fine_position=fine_position, mid_position=mid_position, fine_parent=fine_parent, mid_parent=mid_parent, pair_target=pair_target, pair_source=pair_source, pair_kind=pair_kind)


def extended(pattern, width):
    shape = pattern.shape[:-1] + (SECT, width)
    blocks = pattern.reshape(shape)
    leading = jnp.roll(pattern, HALO, axis=-1).reshape(shape)[..., :HALO]
    trailing = jnp.roll(pattern, -HALO, axis=-1).reshape(shape)[..., width - HALO:]
    return jnp.concatenate([leading, blocks, trailing], axis=-1)


def settle(values):
    return lax.optimization_barrier(values.astype(jnp.bfloat16))


def rotate(pattern, angles):
    cosine = jnp.cos(angles)[:, None, :]
    sine = jnp.sin(angles)[:, None, :]
    real_part = pattern[:, 0]
    imag_part = pattern[:, 1]
    return jnp.stack([cosine * real_part - sine * imag_part, sine * real_part + cosine * imag_part], axis=1)


def translate(coupling, sources):
    highest = lax.Precision.HIGHEST
    real_part = jnp.einsum("tud,urd->trd", coupling[:, :, 0], sources[:, 0], precision=highest) - jnp.einsum("tud,urd->trd", coupling[:, :, 1], sources[:, 1], precision=highest)
    imag_part = jnp.einsum("tud,urd->trd", coupling[:, :, 0], sources[:, 1], precision=highest) + jnp.einsum("tud,urd->trd", coupling[:, :, 1], sources[:, 0], precision=highest)
    return jnp.stack([real_part, imag_part], axis=1)


def reference(fine_pattern, fine_interp, mid_interp, fine_angle, top_angle, translator, fine_position, mid_position, fine_parent, mid_parent, pair_target, pair_source, pair_kind):
    highest = lax.Precision.HIGHEST
    widened_fine = jnp.moveaxis(extended(fine_pattern, FS), 3, 0)
    fine_table = jnp.moveaxis(fine_angle.reshape(POS, SECT, MS), 1, 0)

    def fine_step(inputs):
        widened, matrix, angle_table = inputs
        coarse = settle(jnp.einsum("bcrk,kn->bcrn", widened.astype(jnp.float32), matrix.astype(jnp.float32), precision=highest))
        turned = rotate(coarse.astype(jnp.float32), angle_table[fine_position])
        return jax.ops.segment_sum(turned, fine_parent, num_segments=MBOX).astype(jnp.bfloat16)

    mid_sectors = lax.map(fine_step, (widened_fine, fine_interp, fine_table))
    mid_pattern = jnp.moveaxis(mid_sectors, 0, 3).reshape(MBOX, 2, RHS, MDIR)

    slot_index = pair_target * TBOX + pair_source
    onehot_pair = (slot_index[:, None] == jnp.arange(TBOX * TBOX, dtype=jnp.int32)[None, :]).astype(jnp.float32)
    onehot_kind = (pair_kind[:, None] == jnp.arange(KINDS, dtype=jnp.int32)[None, :]).astype(jnp.float32)
    counts = jnp.dot(onehot_pair.T, onehot_kind, precision=highest).astype(jnp.bfloat16)

    widened_mid = jnp.moveaxis(extended(mid_pattern, MS), 3, 0)
    top_table = jnp.moveaxis(top_angle.reshape(POS, SECT, TS), 1, 0)
    operators = jnp.moveaxis(translator.reshape(KINDS, 2, SECT, TS), 2, 0)

    def top_step(inputs):
        widened, matrix, angle_table, operator_table = inputs
        coarse = settle(jnp.einsum("bcrk,kn->bcrn", widened.astype(jnp.float32), matrix.astype(jnp.float32), precision=highest))
        angles = angle_table[mid_position]
        turned = rotate(coarse.astype(jnp.float32), angles)
        top_pattern = settle(jax.ops.segment_sum(turned, mid_parent, num_segments=TBOX))
        coupling = settle(jnp.dot(counts, operator_table.reshape(KINDS, 2 * TS), preferred_element_type=jnp.float32).reshape(TBOX, TBOX, 2, TS))
        incoming = translate(coupling.astype(jnp.float32), top_pattern.astype(jnp.float32))
        rounded = settle(incoming)
        spread = settle(rotate(rounded.astype(jnp.float32)[mid_parent], -angles))
        contrib = jnp.einsum("bcrn,kn->bcrk", spread.astype(jnp.float32), matrix.astype(jnp.float32), precision=highest)
        return incoming, contrib

    incoming, contrib = lax.map(top_step, (widened_mid, mid_interp, top_table, operators))
    top_incoming = jnp.moveaxis(incoming, 0, 3).reshape(TBOX, 2, RHS, TDIR)
    central = contrib[..., HALO:HALO + MS]
    leading = contrib[..., :HALO]
    trailing = contrib[..., HALO + MS:]
    central = central.at[..., :HALO].add(jnp.roll(trailing, 1, axis=0))
    central = central.at[..., MS - HALO:].add(jnp.roll(leading, -1, axis=0))
    mid_incoming = jnp.moveaxis(central, 0, 3).reshape(MBOX, 2, RHS, MDIR)
    return top_incoming, mid_incoming
```

```python
import functools

import jax
import jax.numpy as jnp
from jax import lax
from jax.experimental import pallas as pl
from jax.experimental.pallas import tpu as pltpu
from jax.sharding import PartitionSpec as P

FS = 256
MS = 896
TS = 3328
HALO = 64
LANES = 128
KIDS = 4
TILE = 256
UNROLL = 4
BF = jnp.bfloat16
F32 = jnp.float32


def params(mib=60):
    return pltpu.CompilerParams(vmem_limit_bytes=mib * 1024 * 1024)


def low_lanes(shape):
    return lax.broadcasted_iota(jnp.int32, shape, len(shape) - 1) < HALO


def pack_kernel(x_ref, o_ref):
    sectors = o_ref.shape[0]
    low = low_lanes(x_ref.shape[1:2] + (LANES,))
    for s in range(sectors):
        o_ref[s, 0, :, :FS] = x_ref[0, :, s * FS : (s + 1) * FS]
        nxt = ((s + 1) % sectors) * FS
        prv = ((s - 1) % sectors) * FS + FS - LANES
        o_ref[s, 0, :, FS:] = jnp.where(
            low, x_ref[0, :, nxt : nxt + LANES], x_ref[0, :, prv : prv + LANES]
        )


def pack(fine, sectors):
    rows, columns, width = fine.shape
    return pl.pallas_call(
        pack_kernel,
        out_shape=jax.ShapeDtypeStruct((sectors, rows, columns, FS + LANES), BF),
        grid=(rows,),
        in_specs=[pl.BlockSpec((1, columns, width), lambda i: (i, 0, 0))],
        out_specs=pl.BlockSpec((sectors, 1, columns, FS + LANES), lambda i: (0, i, 0, 0)),
        compiler_params=params(),
        name="pack",
    )(fine)


def rotate_sum(values, first, position, cos_ref, sin_ref, row):
    real = imag = None
    for j in range(KIDS):
        p = position[first + j]
        c = cos_ref[pl.ds(p, 1), :]
        s = sin_ref[pl.ds(p, 1), :]
        u = values[(row + j) * 32 : (row + j) * 32 + 16]
        v = values[(row + j) * 32 + 16 : (row + j) * 32 + 32]
        re = c * u - s * v
        im = s * u + c * v
        real = re if real is None else real + re
        imag = im if imag is None else imag + im
    return real, imag


def fine_kernel(child, position, x_ref, w_ref, cos_ref, sin_ref, o_ref):
    per = 4

    def body(g, _):
        base = g * (per * KIDS)
        lhs = jnp.concatenate([x_ref[child[base + i]] for i in range(per * KIDS)], axis=0)
        values = jnp.dot(lhs, w_ref[...], preferred_element_type=F32)
        for m in range(per):
            real, imag = rotate_sum(
                values, base + m * KIDS, position, cos_ref, sin_ref, m * KIDS
            )
            o_ref[g * per + m, :16] = real.astype(BF)
            o_ref[g * per + m, 16:] = imag.astype(BF)
        return 0

    lax.fori_loop(0, o_ref.shape[0] // per, body, 0)


def lift_fine(child, position, x, w, cos, sin):
    boxes, rows, k = x.shape
    n = w.shape[1]
    return pl.pallas_call(
        fine_kernel,
        out_shape=jax.ShapeDtypeStruct((boxes // KIDS, rows, n), BF),
        grid_spec=pltpu.PrefetchScalarGridSpec(
            num_scalar_prefetch=2,
            grid=(1,),
            in_specs=[
                pl.BlockSpec((boxes, rows, k), lambda i, *_: (0, 0, 0)),
                pl.BlockSpec((k, n), lambda i, *_: (0, 0)),
                pl.BlockSpec(cos.shape, lambda i, *_: (0, 0)),
                pl.BlockSpec(sin.shape, lambda i, *_: (0, 0)),
            ],
            out_specs=pl.BlockSpec((boxes // KIDS, rows, n), lambda i, *_: (0, 0, 0)),
        ),
        compiler_params=params(),
        cost_estimate=pl.CostEstimate(
            flops=2 * boxes * rows * k * n, bytes_accessed=2 * boxes * rows * k, transcendentals=0
        ),
        name="lift_fine",
    )(child, position, x, w, cos, sin)


def mid_kernel(child, position, e_ref, c_ref, n_ref, p_ref, w_ref, cos_ref, sin_ref, o_ref, lhs):
    boxes, rows, _ = e_ref.shape
    edge = 2 * LANES
    inner = c_ref.shape[2]

    @pl.when(pl.program_id(0) == 0)
    def _():
        low = low_lanes((rows, LANES))

        def gather(i, _):
            m = child[i]
            at = pl.ds(pl.multiple_of(i * rows, rows), rows)
            lhs[at, :edge] = e_ref[m]
            lhs[at, edge : edge + inner] = c_ref[m]
            lhs[at, edge + inner :] = jnp.where(low, n_ref[m], p_ref[m])
            return 0

        lax.fori_loop(0, boxes, gather, 0)

    values = jnp.dot(lhs[...], w_ref[...], preferred_element_type=F32)
    for t in range(boxes // KIDS):
        real, imag = rotate_sum(values, t * KIDS, position, cos_ref, sin_ref, t * KIDS)
        o_ref[t, :16] = real.astype(BF)
        o_ref[t, 16:] = imag.astype(BF)


def lift_mid(child, position, edges, central, from_next, from_prev, w, cos, sin, first, tiles):
    boxes, rows, _ = edges.shape
    k = w.shape[0]
    whole = lambda a: pl.BlockSpec(a.shape, lambda i, *_: (0,) * a.ndim)
    return pl.pallas_call(
        mid_kernel,
        out_shape=jax.ShapeDtypeStruct((boxes // KIDS, rows, tiles * TILE), BF),
        grid_spec=pltpu.PrefetchScalarGridSpec(
            num_scalar_prefetch=2,
            grid=(tiles,),
            in_specs=[
                whole(edges),
                whole(central),
                whole(from_next),
                whole(from_prev),
                pl.BlockSpec((k, TILE), lambda i, *_: (0, i + first)),
                pl.BlockSpec((cos.shape[0], TILE), lambda i, *_: (0, i + first)),
                pl.BlockSpec((sin.shape[0], TILE), lambda i, *_: (0, i + first)),
            ],
            out_specs=pl.BlockSpec((boxes // KIDS, rows, TILE), lambda i, *_: (0, 0, i)),
            scratch_shapes=[pltpu.VMEM((boxes * rows, k), BF)],
        ),
        compiler_params=params(),
        cost_estimate=pl.CostEstimate(
            flops=2 * boxes * rows * k * tiles * TILE,
            bytes_accessed=2 * k * tiles * TILE,
            transcendentals=0,
        ),
        name="lift_mid",
    )(child, position, edges, central, from_next, from_prev, w, cos, sin)


def translate_kernel(
    starts, source, kind, group, child, position, *refs
):
    parts = refs[:4]
    op_ref, cos_ref, sin_ref, top_ref, spread_ref, held = refs[4:]
    group_size = parts[0].shape[0]
    for j in range(4):
        held[pl.ds((group[0] ^ j) * group_size, group_size)] = parts[j][...]

    def target(t, _):
        def pairs(i, carry):
            real, imag = carry
            for n in range(UNROLL):
                at = i * UNROLL + n
                u = source[at]
                k = kind[at]
                xr = held[u, :16].astype(F32)
                xi = held[u, 16:].astype(F32)
                tr = op_ref[k, 0:1, :]
                ti = op_ref[k, 1:2, :]
                real = real + tr * xr - ti * xi
                imag = imag + tr * xi + ti * xr
            return real, imag

        zero = jnp.zeros((16, held.shape[2]), F32)
        real, imag = lax.fori_loop(starts[t], starts[t + 1], pairs, (zero, zero))
        top_ref[t, 0] = real
        top_ref[t, 1] = imag
        real = real.astype(BF).astype(F32)
        imag = imag.astype(BF).astype(F32)
        for j in range(KIDS):
            m = child[t * KIDS + j]
            p = position[t * KIDS + j]
            c = cos_ref[pl.ds(p, 1), :]
            s = sin_ref[pl.ds(p, 1), :]
            spread_ref[m, :16] = (c * real + s * imag).astype(BF)
            spread_ref[m, 16:] = (c * imag - s * real).astype(BF)
        return 0

    lax.fori_loop(0, group_size, target, 0)


def translate(starts, source, kind, group, child, position, parts, operators, cos, sin):
    size, rows, width = parts[0].shape
    mids = size * KIDS
    tiles = width // TILE
    part = pl.BlockSpec((size, rows, TILE), lambda i, *_: (0, 0, i))
    return pl.pallas_call(
        translate_kernel,
        out_shape=(
            jax.ShapeDtypeStruct((size, 2, rows // 2, width), F32),
            jax.ShapeDtypeStruct((mids, rows, width), BF),
        ),
        grid_spec=pltpu.PrefetchScalarGridSpec(
            num_scalar_prefetch=6,
            grid=(tiles,),
            in_specs=[part] * 4
            + [
                pl.BlockSpec(operators.shape[:2] + (TILE,), lambda i, *_: (0, 0, i)),
                pl.BlockSpec((cos.shape[0], TILE), lambda i, *_: (0, i)),
                pl.BlockSpec((sin.shape[0], TILE), lambda i, *_: (0, i)),
            ],
            out_specs=(
                pl.BlockSpec((size, 2, rows // 2, TILE), lambda i, *_: (0, 0, 0, i)),
                pl.BlockSpec((mids, rows, TILE), lambda i, *_: (0, 0, i)),
            ),
            scratch_shapes=[pltpu.VMEM((4 * size, rows, TILE), BF)],
        ),
        compiler_params=params(),
        name="translate",
    )(starts, source, kind, group, child, position, *parts, operators, cos, sin)


def edge_kernel(x_ref, p_ref, n_ref, o_ref):
    low = low_lanes(p_ref.shape)
    first = pl.program_id(0) == 0
    take = jnp.where(first, p_ref[...].astype(F32), n_ref[...].astype(F32))
    o_ref[...] = x_ref[...] + jnp.where(low == first, take, 0.0)


def add_edges(central, from_prev, from_next):
    boxes, rows, width = central.shape
    last = width // LANES - 1
    tile = pl.BlockSpec((boxes, rows, LANES), lambda i: (0, 0, i * last))
    halo = pl.BlockSpec((boxes, rows, LANES), lambda i: (0, 0, 0))
    return pl.pallas_call(
        edge_kernel,
        out_shape=jax.ShapeDtypeStruct(central.shape, F32),
        grid=(2,),
        in_specs=[tile, halo, halo],
        out_specs=tile,
        input_output_aliases={0: 0},
        compiler_params=params(),
        name="add_edges",
    )(central, from_prev, from_next)


def children_of(parents, positions, count):
    n = parents.shape[0]
    index = jnp.arange(n, dtype=jnp.int32)
    before = (parents[None, :] < parents[:, None]) | (
        (parents[None, :] == parents[:, None]) & (index[None, :] < index[:, None])
    )
    rank = jnp.sum(before.astype(jnp.int32), axis=1)
    match = (rank[None, :] == index[:, None]).astype(jnp.int32)
    return (
        jnp.sum(match * index[None, :], axis=1),
        jnp.sum(match * positions[None, :], axis=1),
    )


def pair_lists(target, source, kind, base, count, kinds):
    pairs = target.shape[0]
    index = jnp.arange(pairs, dtype=jnp.int32)
    local = target - base
    boxes = jnp.arange(count, dtype=jnp.int32)
    mine = local[None, :] == boxes[:, None]
    padded = (jnp.sum(mine.astype(jnp.int32), axis=1) + UNROLL - 1) // UNROLL
    starts = jnp.sum(
        jnp.where(
            boxes[None, :] < jnp.arange(count + 1, dtype=jnp.int32)[:, None], padded[None, :], 0
        ),
        axis=1,
    )
    earlier = (local[None, :] == local[:, None]) & (index[None, :] < index[:, None])
    within = jnp.sum(earlier.astype(jnp.int32), axis=1)
    begin = jnp.sum(jnp.where(mine, starts[:count, None] * UNROLL, 0), axis=0)
    slot = jnp.where(jnp.any(mine, axis=0), begin + within, -1)
    slots = pairs + count * (UNROLL - 1)
    match = (slot[None, :] == jnp.arange(slots, dtype=jnp.int32)[:, None]).astype(jnp.int32)
    return (
        starts,
        jnp.sum(match * source[None, :], axis=1),
        kinds + jnp.sum(match * (kind - kinds)[None, :], axis=1),
    )


def per_device(
    fine_pattern,
    fine_interp,
    mid_interp,
    fine_angle,
    top_angle,
    translator,
    fine_position,
    mid_position,
    fine_parent,
    mid_parent,
    pair_target,
    pair_source,
    pair_kind,
):
    box = lax.axis_index("box")
    dirs = lax.axis_size("dir")
    fine_local, _, columns, width = fine_pattern.shape
    rows = 2 * columns
    fine_group = fine_local * dirs
    mid_group = fine_group // KIDS
    top_group = mid_group // KIDS
    kinds = translator.shape[0]
    up = [(i, (i + 1) % dirs) for i in range(dirs)]
    down = [((i + 1) % dirs, i) for i in range(dirs)]

    packed = pack(fine_pattern.reshape(fine_local * 2, columns, width), dirs)
    arrived = lax.all_to_all(packed, "dir", split_axis=0, concat_axis=0, tiled=True)
    arrived = arrived.reshape(fine_group, rows, FS + LANES)

    cut = lambda a, n: lax.dynamic_slice_in_dim(a, box * n, n)
    fine_child, fine_pos = children_of(
        cut(fine_parent, fine_group), cut(fine_position, fine_group), mid_group
    )
    mid_child, mid_pos = children_of(
        cut(mid_parent, mid_group), cut(mid_position, mid_group), top_group
    )
    starts, source, kind = pair_lists(
        pair_target, pair_source, pair_kind, box * top_group, top_group, kinds
    )
    fine_cos, fine_sin = jnp.cos(fine_angle), jnp.sin(fine_angle)
    top_cos, top_sin = jnp.cos(top_angle), jnp.sin(top_angle)
    operators = jnp.concatenate(
        [translator.astype(F32), jnp.zeros((8,) + translator.shape[1:], F32)], axis=0
    )
    wf = fine_interp[0]
    wf = jnp.concatenate([wf[HALO : HALO + FS], wf[HALO + FS :], wf[:HALO]], axis=0)
    wm = mid_interp[0]
    last = HALO + MS - LANES
    wm_halo = jnp.concatenate([wm[HALO + MS :], wm[:HALO]], axis=0)
    wm_central = wm[HALO : HALO + MS]
    wm_up = jnp.concatenate(
        [wm[HALO : HALO + LANES], wm[last : HALO + MS], wm[HALO + LANES : last], wm_halo], axis=0
    )
    ends = lambda a: jnp.concatenate([a[:, :LANES], a[:, MS - LANES :]], axis=1)
    inside = lambda a: a[:, LANES : MS - LANES]

    edges = lift_fine(fine_child, fine_pos, arrived, ends(wf), ends(fine_cos), ends(fine_sin))
    from_next = lax.ppermute(edges[:, :, :LANES], "dir", down)
    from_prev = lax.ppermute(edges[:, :, LANES:], "dir", up)
    central = lift_fine(
        fine_child, fine_pos, arrived, inside(wf), inside(fine_cos), inside(fine_sin)
    )
    top = lift_mid(
        mid_child, mid_pos, edges, central, from_next, from_prev, wm_up, top_cos, top_sin, 0,
        TS // TILE,
    )
    core = [(i, i ^ 1) for i in range(4)]
    far = [(i, i ^ 2) for i in range(4)]
    top_core = lax.ppermute(top, "box", core)
    top_far = lax.ppermute(top, "box", far)
    top_both = lax.ppermute(top_far, "box", core)
    top_incoming, spread = translate(
        starts, source, kind, box[None], mid_child, mid_pos,
        (top, top_core, top_far, top_both), operators, top_cos, top_sin,
    )
    halo = jnp.einsum("bxn,kn->bxk", spread, wm_halo, preferred_element_type=F32).astype(BF)
    below = lax.ppermute(halo, "dir", up)
    above = lax.ppermute(halo, "dir", down)
    middle = jnp.einsum("bxn,kn->bxk", spread, wm_central, preferred_element_type=F32)
    mid_incoming = add_edges(middle, below, above)
    return top_incoming, mid_incoming.reshape(mid_group, 2, columns, MS)


def solution(mesh):
    placed = (
        P(("box", "dir"), None, None, None),
        P("dir", None, None),
        P("dir", None, None),
        P(None, "dir"),
        P(None, "dir"),
        P(None, None, "dir"),
        P(),
        P(),
        P(),
        P(),
        P(),
        P(),
        P(),
    )
    return jax.shard_map(
        per_device,
        mesh=mesh,
        in_specs=placed,
        out_specs=(P("box", None, None, "dir"), P("box", None, None, "dir")),
        check_vma=False,
    )
```

```python
import jax
import jax.numpy as jnp
from jax import lax
from jax.experimental import pallas as pl
from jax.experimental.pallas import tpu as pltpu
from jax.sharding import PartitionSpec as P


FS = 256
MS = 896
HALO = 64
LANES = 128
KIDS = 4
TILE = 256
UNROLL = 4
CHUNKS = (2, 4, 4, 3)
BF = jnp.bfloat16
F32 = jnp.float32


def params(mib):
    return pltpu.CompilerParams(vmem_limit_bytes=mib * 1024 * 1024)


def low_lanes(shape):
    return lax.broadcasted_iota(jnp.int32, shape, len(shape) - 1) < HALO


def pack_kernel(x_hbm, o_hbm, x_ref, o_ref, in_sem, out_sem):
    rows, columns, _ = x_ref.shape
    sectors = o_ref.shape[1]
    low = low_lanes((columns, LANES))
    loads = [pltpu.make_async_copy(x_hbm.at[i], x_ref.at[i], in_sem.at[i]) for i in range(rows)]
    stores = [
        pltpu.make_async_copy(o_ref.at[i], o_hbm.at[:, i], out_sem.at[i]) for i in range(rows)
    ]
    for load in loads:
        load.start()
    for i in range(rows):
        loads[i].wait()
        for s in range(sectors):
            o_ref[i, s, :, :FS] = x_ref[i, :, s * FS : (s + 1) * FS]
            nxt = ((s + 1) % sectors) * FS
            prv = ((s - 1) % sectors) * FS + FS - LANES
            o_ref[i, s, :, FS:] = jnp.where(
                low, x_ref[i, :, nxt : nxt + LANES], x_ref[i, :, prv : prv + LANES]
            )
        stores[i].start()
    for store in stores:
        store.wait()


def pack(fine, sectors):
    rows, columns, width = fine.shape
    return pl.pallas_call(
        pack_kernel,
        out_shape=jax.ShapeDtypeStruct((sectors, rows, columns, FS + LANES), BF),
        in_specs=[pl.BlockSpec(memory_space=pl.ANY)],
        out_specs=pl.BlockSpec(memory_space=pl.ANY),
        scratch_shapes=[
            pltpu.VMEM((rows, columns, width), BF),
            pltpu.VMEM((rows, sectors, columns, FS + LANES), BF),
            pltpu.SemaphoreType.DMA((rows,)),
            pltpu.SemaphoreType.DMA((rows,)),
        ],
        compiler_params=params(8),
        name="pack",
    )(fine)


def rotate_sum(values, first, position, cos_ref, sin_ref, row):
    real = imag = None
    for j in range(KIDS):
        p = position[first + j]
        c = cos_ref[pl.ds(p, 1), :]
        s = sin_ref[pl.ds(p, 1), :]
        u = values[(row + j) * 32 : (row + j) * 32 + 16]
        v = values[(row + j) * 32 + 16 : (row + j) * 32 + 32]
        re = c * u - s * v
        im = s * u + c * v
        real = re if real is None else real + re
        imag = im if imag is None else imag + im
    return real, imag


def swap(tile):
    return pltpu.roll(tile, HALO, axis=1)


GROUP = 4


def fine_kernel(child, position, slot, x_hbm, w_ref, cos_ref, sin_ref, o_ref, *rest):
    lhs, sem = rest[-2:]
    halos = rest[:-2]
    mids, rows, _ = o_ref.shape
    per = GROUP * KIDS
    groups = mids // GROUP
    span = per * rows

    def fetch(g, _):
        for i in range(per):
            pltpu.make_async_copy(
                x_hbm.at[child[g * per + i]], lhs.at[g * per + i], sem.at[g]
            ).start()
        return 0

    lax.fori_loop(0, groups, fetch, 0)
    low = low_lanes((rows // 2, LANES))

    def body(g, _):
        base = g * per
        pltpu.make_async_copy(x_hbm.at[pl.ds(0, per)], lhs.at[pl.ds(base, per)], sem.at[g]).wait()
        block = lhs[pl.ds(base, per)].reshape(span, lhs.shape[2])
        values = jnp.dot(block, w_ref[...], preferred_element_type=F32)
        for m in range(GROUP):
            real, imag = rotate_sum(
                values, base + m * KIDS, position, cos_ref, sin_ref, m * KIDS
            )
            at = slot[g * GROUP + m]
            o_ref[at, :16] = real.astype(BF)
            o_ref[at, 16:] = imag.astype(BF)
            if halos:
                head, tail = real[:, :LANES], imag[:, :LANES]
                halos[0][at] = jnp.where(low, head, swap(tail)).astype(BF)
                head, tail = real[:, LANES:], imag[:, LANES:]
                halos[1][at] = jnp.where(low, swap(head), tail).astype(BF)
        return 0

    lax.fori_loop(0, groups, body, 0)


def lift_fine(child, position, slot, x, w, cos, sin, with_halos):
    boxes, rows, k = x.shape
    mids = boxes // KIDS
    n = w.shape[1]
    whole = lambda shape: pl.BlockSpec(shape, lambda i, *_: (0,) * len(shape))
    shapes = [(mids, rows, n)] + [(mids, rows // 2, LANES)] * (2 if with_halos else 0)
    return pl.pallas_call(
        fine_kernel,
        out_shape=[jax.ShapeDtypeStruct(shape, BF) for shape in shapes],
        grid_spec=pltpu.PrefetchScalarGridSpec(
            num_scalar_prefetch=3,
            grid=(1,),
            in_specs=[
                pl.BlockSpec(memory_space=pl.ANY),
                whole((k, n)),
                whole(cos.shape),
                whole(sin.shape),
            ],
            out_specs=[whole(shape) for shape in shapes],
            scratch_shapes=[
                pltpu.VMEM((boxes, rows, k), BF),
                pltpu.SemaphoreType.DMA((mids // GROUP,)),
            ],
        ),
        compiler_params=params(14),
        cost_estimate=pl.CostEstimate(
            flops=2 * boxes * rows * k * n, bytes_accessed=2 * boxes * rows * k, transcendentals=0
        ),
        name="lift_fine",
    )(child, position, slot, x, w, cos, sin)


def mid_kernel(position, e_ref, c_ref, n_ref, p_ref, w_ref, cos_ref, sin_ref, o_ref, lhs):
    boxes, rows, _ = e_ref.shape
    half = rows // 2
    edge = 2 * LANES
    inner = c_ref.shape[2]

    @pl.when(pl.program_id(0) == 0)
    def _():
        low = low_lanes((half, LANES))
        lhs[:, :edge] = e_ref[...].reshape(boxes * rows, edge)
        lhs[:, edge : edge + inner] = c_ref[...].reshape(boxes * rows, inner)
        for m in range(boxes):
            nxt = n_ref[m].astype(F32)
            prv = p_ref[m].astype(F32)
            real = jnp.where(low, nxt, swap(prv))
            imag = jnp.where(low, swap(nxt), prv)
            lhs[m * rows : m * rows + half, edge + inner :] = real.astype(BF)
            lhs[m * rows + half : (m + 1) * rows, edge + inner :] = imag.astype(BF)

    values = jnp.dot(lhs[...], w_ref[...], preferred_element_type=F32)
    for t in range(boxes // KIDS):
        real, imag = rotate_sum(values, t * KIDS, position, cos_ref, sin_ref, t * KIDS)
        o_ref[t, :16] = real.astype(BF)
        o_ref[t, 16:] = imag.astype(BF)


def lift_mid(position, edges, central, from_next, from_prev, w, cos, sin, first, tiles):
    boxes, rows, _ = edges.shape
    k = w.shape[0]
    whole = lambda a: pl.BlockSpec(a.shape, lambda i, *_: (0,) * a.ndim)
    return pl.pallas_call(
        mid_kernel,
        out_shape=jax.ShapeDtypeStruct((boxes // KIDS, rows, tiles * TILE), BF),
        grid_spec=pltpu.PrefetchScalarGridSpec(
            num_scalar_prefetch=1,
            grid=(tiles,),
            in_specs=[
                whole(edges),
                whole(central),
                whole(from_next),
                whole(from_prev),
                pl.BlockSpec((k, TILE), lambda i, *_: (0, i + first)),
                pl.BlockSpec((cos.shape[0], TILE), lambda i, *_: (0, i + first)),
                pl.BlockSpec((sin.shape[0], TILE), lambda i, *_: (0, i + first)),
            ],
            out_specs=pl.BlockSpec((boxes // KIDS, rows, TILE), lambda i, *_: (0, 0, i)),
            scratch_shapes=[pltpu.VMEM((boxes * rows, k), BF)],
        ),
        compiler_params=params(14),
        cost_estimate=pl.CostEstimate(
            flops=2 * boxes * rows * k * tiles * TILE,
            bytes_accessed=2 * k * tiles * TILE,
            transcendentals=0,
        ),
        name="lift_mid",
    )(position, edges, central, from_next, from_prev, w, cos, sin)


def accumulate(t, starts, source, kind, held, op_ref, initial):
    def pairs(i, carry):
        real, imag = carry
        for n in range(UNROLL):
            at = i * UNROLL + n
            u = source[at]
            k = kind[at]
            xr = held[u, :16].astype(F32)
            xi = held[u, 16:].astype(F32)
            tr = op_ref[k, 0:1, :]
            ti = op_ref[k, 1:2, :]
            real = real + tr * xr - ti * xi
            imag = imag + tr * xi + ti * xr
        return real, imag

    return lax.fori_loop(starts[t], starts[t + 1], pairs, initial)


def near_kernel(starts, source, kind, a_ref, b_ref, op_ref, o_ref, held):
    size = a_ref.shape[0]
    held[:size] = a_ref[...]
    held[size:] = b_ref[...]

    def target(t, _):
        zero = jnp.zeros((16, held.shape[2]), F32)
        real, imag = accumulate(t, starts, source, kind, held, op_ref, (zero, zero))
        o_ref[t, 0] = real
        o_ref[t, 1] = imag
        return 0

    lax.fori_loop(0, size, target, 0)


def translate_near(lists, own, core, operators, first, tiles):
    size, rows, _ = own.shape
    part = pl.BlockSpec((size, rows, TILE), lambda i, *_: (0, 0, i))
    return pl.pallas_call(
        near_kernel,
        out_shape=jax.ShapeDtypeStruct((size, 2, rows // 2, tiles * TILE), F32),
        grid_spec=pltpu.PrefetchScalarGridSpec(
            num_scalar_prefetch=3,
            grid=(tiles,),
            in_specs=[
                part,
                part,
                pl.BlockSpec(operators.shape[:2] + (TILE,), lambda i, *_: (0, 0, i + first)),
            ],
            out_specs=pl.BlockSpec((size, 2, rows // 2, TILE), lambda i, *_: (0, 0, 0, i)),
            scratch_shapes=[pltpu.VMEM((2 * size, rows, TILE), BF)],
        ),
        compiler_params=params(6),
        cost_estimate=pl.CostEstimate(
            flops=2 * size * rows * 512 * tiles * TILE // 8,
            bytes_accessed=16 * size * rows * tiles * TILE,
            transcendentals=0,
        ),
        name="translate_near",
    )(*lists, own, core, operators)


def far_kernel(
    starts, source, kind, child, position, a_ref, b_ref, near_ref, op_ref, cos_ref, sin_ref, *rest
):
    top_ref, spread_ref, held = rest[-3:]
    size = a_ref.shape[0]
    held[:size] = a_ref[...]
    held[size:] = b_ref[...]

    def target(t, _):
        real, imag = accumulate(
            t, starts, source, kind, held, op_ref, (near_ref[t, 0], near_ref[t, 1])
        )
        top_ref[t, 0] = real
        top_ref[t, 1] = imag
        real = real.astype(BF).astype(F32)
        imag = imag.astype(BF).astype(F32)
        for j in range(KIDS):
            m = child[t * KIDS + j]
            p = position[t * KIDS + j]
            c = cos_ref[pl.ds(p, 1), :]
            s = sin_ref[pl.ds(p, 1), :]
            spread_ref[m, :16] = (c * real + s * imag).astype(BF)
            spread_ref[m, 16:] = (c * imag - s * real).astype(BF)
        return 0

    lax.fori_loop(0, size, target, 0)


def translate_far(lists, child, position, far, both, near, operators, cos, sin, held, first, tiles):
    size, rows, _ = far.shape
    mids = size * KIDS
    width = cos.shape[1]
    part = pl.BlockSpec((size, rows, TILE), lambda i, *_: (0, 0, i))
    wide = lambda a: pl.BlockSpec((a.shape[0], TILE), lambda i, *_: (0, i + first))
    extra = [] if held is None else [held]
    return pl.pallas_call(
        far_kernel,
        out_shape=(
            jax.ShapeDtypeStruct((size, 2, rows // 2, width), F32),
            jax.ShapeDtypeStruct((mids, rows, tiles * TILE), BF),
        ),
        grid_spec=pltpu.PrefetchScalarGridSpec(
            num_scalar_prefetch=5,
            grid=(tiles,),
            in_specs=[
                part,
                part,
                pl.BlockSpec((size, 2, rows // 2, TILE), lambda i, *_: (0, 0, 0, i)),
                pl.BlockSpec(operators.shape[:2] + (TILE,), lambda i, *_: (0, 0, i + first)),
                wide(cos),
                wide(sin),
            ]
            + [pl.BlockSpec(memory_space=pl.ANY)] * len(extra),
            out_specs=(
                pl.BlockSpec((size, 2, rows // 2, TILE), lambda i, *_: (0, 0, 0, i + first)),
                pl.BlockSpec((mids, rows, TILE), lambda i, *_: (0, 0, i)),
            ),
            scratch_shapes=[pltpu.VMEM((2 * size, rows, TILE), BF)],
        ),
        input_output_aliases={} if held is None else {11: 0},
        compiler_params=params(8),
        cost_estimate=pl.CostEstimate(
            flops=2 * size * rows * 512 * tiles * TILE // 8,
            bytes_accessed=16 * size * rows * tiles * TILE,
            transcendentals=0,
        ),
        name="translate_far",
    )(*lists, child, position, far, both, near, operators, cos, sin, *extra)


def halo_kernel(x_ref, w_ref, before_ref, up_ref, down_ref):
    boxes, rows, _ = x_ref.shape
    half = rows // 2
    low = low_lanes((half, LANES))
    values = lax.dot_general(
        x_ref[...].reshape(boxes * rows, x_ref.shape[2]),
        w_ref[...],
        (((1,), (1,)), ((), ())),
        preferred_element_type=F32,
    )
    for m in range(boxes):
        real = values[m * rows : m * rows + half] + before_ref[m, :half]
        imag = values[m * rows + half : (m + 1) * rows] + before_ref[m, half:]
        up_ref[m] = jnp.where(low, real, swap(imag)).astype(BF)
        down_ref[m] = jnp.where(low, swap(real), imag).astype(BF)


def halo_out(spread, w, before):
    boxes, rows, _ = spread.shape
    shape = jax.ShapeDtypeStruct((boxes, rows // 2, LANES), BF)
    return pl.pallas_call(
        halo_kernel,
        out_shape=(shape, shape),
        compiler_params=params(8),
        name="halo_out",
    )(spread, w, before)


def edge_kernel(x_ref, p_ref, n_ref, o_ref):
    boxes, rows, _ = x_ref.shape
    half = rows // 2
    low = low_lanes((half, LANES))

    def add(from_prev):
        for m in range(boxes):
            halo = (p_ref if from_prev else n_ref)[m].astype(F32)
            turned = swap(halo)
            real, imag = (halo, turned) if from_prev else (turned, halo)
            keep = low == from_prev
            o_ref[m, :half] = x_ref[m, :half] + jnp.where(keep, real, 0.0)
            o_ref[m, half:] = x_ref[m, half:] + jnp.where(keep, imag, 0.0)

    @pl.when(pl.program_id(0) == 0)
    def _():
        add(True)

    @pl.when(pl.program_id(0) == 1)
    def _():
        add(False)


def add_edges(central, from_prev, from_next):
    boxes, rows, width = central.shape
    last = width // LANES - 1
    tile = pl.BlockSpec((boxes, rows, LANES), lambda i: (0, 0, i * last))
    halo = pl.BlockSpec((boxes, rows // 2, LANES), lambda i: (0, 0, 0))
    return pl.pallas_call(
        edge_kernel,
        out_shape=jax.ShapeDtypeStruct(central.shape, F32),
        grid=(2,),
        in_specs=[tile, halo, halo],
        out_specs=tile,
        input_output_aliases={0: 0},
        compiler_params=params(4),
        name="add_edges",
    )(central, from_prev, from_next)


def children_of(parents, positions):
    n = parents.shape[0]
    index = jnp.arange(n, dtype=jnp.int32)
    before = (parents[None, :] < parents[:, None]) | (
        (parents[None, :] == parents[:, None]) & (index[None, :] < index[:, None])
    )
    rank = jnp.sum(before.astype(jnp.int32), axis=1)
    match = (rank[None, :] == index[:, None]).astype(jnp.int32)
    return (
        jnp.sum(match * index[None, :], axis=1),
        jnp.sum(match * positions[None, :], axis=1),
        rank,
    )


def pair_lists(target, source, kind, take, base, count, kinds):
    pairs = target.shape[0]
    index = jnp.arange(pairs, dtype=jnp.int32)
    local = jnp.where(take, target - base, -1)
    boxes = jnp.arange(count, dtype=jnp.int32)
    mine = local[None, :] == boxes[:, None]
    padded = (jnp.sum(mine.astype(jnp.int32), axis=1) + UNROLL - 1) // UNROLL
    starts = jnp.sum(
        jnp.where(
            boxes[None, :] < jnp.arange(count + 1, dtype=jnp.int32)[:, None], padded[None, :], 0
        ),
        axis=1,
    )
    earlier = (local[None, :] == local[:, None]) & (index[None, :] < index[:, None])
    within = jnp.sum(earlier.astype(jnp.int32), axis=1)
    begin = jnp.sum(jnp.where(mine, starts[:count, None] * UNROLL, 0), axis=0)
    slot = jnp.where(jnp.any(mine, axis=0), begin + within, -1)
    slots = pairs + count * (UNROLL - 1)
    match = (slot[None, :] == jnp.arange(slots, dtype=jnp.int32)[:, None]).astype(jnp.int32)
    return (
        starts,
        jnp.sum(match * source[None, :], axis=1),
        kinds + jnp.sum(match * (kind - kinds)[None, :], axis=1),
    )


def per_device(
    fine_pattern,
    fine_interp,
    mid_interp,
    fine_angle,
    top_angle,
    translator,
    fine_position,
    mid_position,
    fine_parent,
    mid_parent,
    pair_target,
    pair_source,
    pair_kind,
):
    box = lax.axis_index("box")
    dirs = lax.axis_size("dir")
    fine_local, _, columns, width = fine_pattern.shape
    rows = 2 * columns
    fine_group = fine_local * dirs
    mid_group = fine_group // KIDS
    top_group = mid_group // KIDS
    kinds = translator.shape[0]
    up = [(i, (i + 1) % dirs) for i in range(dirs)]
    down = [((i + 1) % dirs, i) for i in range(dirs)]

    packed = pack(fine_pattern.reshape(fine_local * 2, columns, width), dirs)
    arrived = lax.all_to_all(packed, "dir", split_axis=0, concat_axis=0, tiled=True)
    arrived = arrived.reshape(fine_group, rows, FS + LANES)

    cut = lambda a, n: lax.dynamic_slice_in_dim(a, box * n, n)
    fine_child, fine_pos, _ = children_of(
        cut(fine_parent, fine_group), cut(fine_position, fine_group)
    )
    mid_child, mid_pos, mid_slot = children_of(
        cut(mid_parent, mid_group), cut(mid_position, mid_group)
    )
    away = (pair_source // top_group) ^ box
    slot = (away & 1) * top_group + pair_source % top_group
    near_lists = pair_lists(
        pair_target, slot, pair_kind, away < 2, box * top_group, top_group, kinds
    )
    far_lists = pair_lists(
        pair_target, slot, pair_kind, away >= 2, box * top_group, top_group, kinds
    )
    fine_cos, fine_sin = jnp.cos(fine_angle), jnp.sin(fine_angle)
    top_cos, top_sin = jnp.cos(top_angle), jnp.sin(top_angle)
    operators = jnp.concatenate(
        [translator.astype(F32), jnp.zeros((8,) + translator.shape[1:], F32)], axis=0
    )
    wf = fine_interp[0]
    wf = jnp.concatenate([wf[HALO : HALO + FS], wf[HALO + FS :], wf[:HALO]], axis=0)
    wm = mid_interp[0]
    last = HALO + MS - LANES
    wm_halo = jnp.concatenate([wm[HALO + MS :], wm[:HALO]], axis=0)
    wm_central = wm[HALO : HALO + MS]
    wm_up = jnp.concatenate(
        [wm[HALO : HALO + LANES], wm[last : HALO + MS], wm[HALO + LANES : last], wm_halo], axis=0
    )
    ends = lambda a: jnp.concatenate([a[:, :LANES], a[:, MS - LANES :]], axis=1)
    inside = lambda a: a[:, LANES : MS - LANES]

    edges, head, tail = lift_fine(
        fine_child, fine_pos, mid_slot, arrived, ends(wf), ends(fine_cos), ends(fine_sin), True
    )
    from_next = lax.ppermute(head, "dir", down)
    from_prev = lax.ppermute(tail, "dir", up)
    (central,) = lift_fine(
        fine_child, fine_pos, mid_slot, arrived, inside(wf), inside(fine_cos), inside(fine_sin),
        False,
    )
    core = [(i, i ^ 1) for i in range(4)]
    opposite = [(i, i ^ 2) for i in range(4)]
    far, both, near = [], [], []
    firsts = [sum(CHUNKS[:c]) for c in range(len(CHUNKS))]
    for c, tiles in enumerate(CHUNKS):
        own = lift_mid(
            mid_pos, edges, central, from_next, from_prev, wm_up, top_cos, top_sin,
            firsts[c], tiles,
        )
        far.append(lax.ppermute(own, "box", opposite))
        beside = lax.ppermute(own, "box", core)
        both.append(lax.ppermute(far[-1], "box", core))
        near.append(translate_near(near_lists, own, beside, operators, firsts[c], tiles))
    top_incoming = None
    middle = jnp.zeros((mid_group, rows, MS), F32)
    outer = jnp.zeros((mid_group, rows, LANES), F32)
    for c, tiles in enumerate(CHUNKS):
        top_incoming, spread = translate_far(
            far_lists, mid_child, mid_pos, far[c], both[c], near[c], operators, top_cos,
            top_sin, top_incoming, firsts[c], tiles,
        )
        at = slice(firsts[c] * TILE, (firsts[c] + tiles) * TILE)
        if c + 1 < len(CHUNKS):
            outer += jnp.einsum("bxn,kn->bxk", spread, wm_halo[:, at], preferred_element_type=F32)
        else:
            to_next, to_prev = halo_out(spread, wm_halo[:, at], outer)
            below = lax.ppermute(to_next, "dir", up)
            above = lax.ppermute(to_prev, "dir", down)
        middle += jnp.einsum("bxn,kn->bxk", spread, wm_central[:, at], preferred_element_type=F32)
    mid_incoming = add_edges(middle, below, above)
    return top_incoming, mid_incoming.reshape(mid_group, 2, columns, MS)


def solution(mesh):
    placed = (
        P(("box", "dir"), None, None, None),
        P("dir", None, None),
        P("dir", None, None),
        P(None, "dir"),
        P(None, "dir"),
        P(None, None, "dir"),
        P(),
        P(),
        P(),
        P(),
        P(),
        P(),
        P(),
    )

    return jax.shard_map(
        per_device,
        mesh=mesh,
        in_specs=placed,
        out_specs=(P("box", None, None, "dir"), P("box", None, None, "dir")),
        check_vma=False,
    )
```
